32 devices in a mesh: tm: 4 (over y, core), space: 8 (over z, x).
Axes of the slice: x: 2, y: 2, z: 4, core: 2. Of those that a mesh axis runs over, the one named last changes fastest.
Arguments:
- patches: bfloat16 [16, 128, 512], P('tm', 'space'), may hold values from -6 to 6
- owner_list: int32 [128], replicated, may hold values from 0 to 7, as said below
- valid_rows: int32 [128], replicated, may hold values from 1 to 8, as said below
- embed_weight: bfloat16 [64, 3072], replicated, may hold values from -0.75 to 0.75
- embed_bias: float32 [3072], replicated, may hold values from -3 to 3
- norm_gain: float32 [4, 3072], replicated, may hold values from 0.5 to 1.5
- conv_kernel: float32 [4, 3, 3072], replicated, may hold values from -3 to 3
- conv_bias: float32 [4, 3072], replicated, may hold values from -3 to 3
Outputs:
- packed: bfloat16 [16, 256, 8, 3072], P('tm', 'space')
The draws below stay inside these ranges and needn't reach their ends.
Inputs may be any that keep to these rules, and one draw needn't show every extreme that they name: `owner_list`: among the tiles of one source device (tiles s * 16 to (s + 1) * 16 - 1) no owner appears more than 4 times; some owner appears exactly 4 times among the tiles of every source device, so it receives 2 * 16 tiles. `valid_rows`: some tile has all 8 rows live.
All inputs are finite; a program needn't handle non-finite values.
Results may differ from the reference program's by a relative error of at most 0.009.
Values may be sent and summed in bfloat16 or wider, within the bound.
No kernel may reach another device: no remote copies, remote signals or barrier semaphores. Data moves between devices by JAX's collectives and lax.ppermute only.
A program may use at most 64 MiB of HBM per device.

```python
import jax
import jax.numpy as jnp
from jax import lax

D = 3072
PF = 64
LAYERS = 4
TILES_DEV = 16
TILE_ROWS = 8
FRAMES = 16
TILES = 128
SEND_MOST = 4
SLOTS = 256
N_SPACE = 8


def draw_owner_list(key, part):
    sources = TILES // TILES_DEV
    per_pair = 2 * TILES_DEV // sources
    hot_owner = jax.random.randint(jax.random.fold_in(key, 7), (), 0, sources)

    def one_source(source_index):
        source_key = jax.random.fold_in(key, source_index + 100)
        shuffled = jax.random.permutation(jax.random.fold_in(source_key, 1), sources - 1).astype(jnp.int32)
        others = shuffled + (shuffled >= hot_owner).astype(jnp.int32)
        remaining = jnp.arange(TILES_DEV - per_pair, dtype=jnp.int32) // per_pair
        chosen = jnp.concatenate([jnp.full((per_pair,), 1, jnp.int32) * hot_owner, others[remaining]])
        mixing = jax.random.permutation(jax.random.fold_in(source_key, 2), TILES_DEV)
        return chosen[mixing]
    return jax.vmap(one_source)(jnp.arange(sources, dtype=jnp.int32)).reshape(TILES).astype(jnp.int32)


def draw_valid_rows(key, part):
    counts = jax.random.randint(key, (TILES,), 1, TILE_ROWS + 1)
    full_at = jax.random.randint(jax.random.fold_in(key, 3), (), 0, TILES)
    return jnp.where(jnp.arange(TILES) == full_at, TILE_ROWS, counts).astype(jnp.int32)


def block_levels(key, dims, shards, low, largest):
    factor_of, own = 1.0, jax.random.fold_in(key, 6)
    for position, shards_of in shards:
        draws = jnp.exp(jax.random.uniform(jax.random.fold_in(own, position), (shards_of,), jnp.float32, low / len(shards), largest / len(shards)))
        factor_of = factor_of * jnp.repeat(draws, dims[position] // shards_of).reshape([-1 if axis == position else 1 for axis in range(len(dims))])
    return factor_of


def gaussian(key, dims, scale, limit, pieces=(), held_as=jnp.bfloat16):
    entries = scale * jax.random.normal(key, dims, jnp.float32)
    if pieces:
        entries = entries * block_levels(key, dims, pieces, -0.22, 0.18)
    return jnp.clip(entries, -limit, limit).astype(held_as)


def setup_inputs(seed: int = 0) -> dict:
    keys = jax.random.split(jax.random.key(seed), 9)
    return {
        "patches": gaussian(keys[0], (FRAMES, TILES, TILE_ROWS * PF), 1.0, 6.0, ((0, 4), (1, 8))),
        "owner_list": draw_owner_list(jax.random.fold_in(keys[8], 71), 0),
        "valid_rows": draw_valid_rows(jax.random.fold_in(keys[8], 71), 0),
        "embed_weight": gaussian(keys[3], (PF, D), PF ** -0.5, 0.75),
        "embed_bias": gaussian(keys[4], (D,), 0.5, 3.0, (), jnp.float32),
        "norm_gain": jnp.clip(1.0 + 0.1 * jax.random.normal(keys[5], (LAYERS, D), jnp.float32), 0.5, 1.5),
        "conv_kernel": gaussian(keys[6], (LAYERS, 3, D), 0.6, 3.0, (), jnp.float32),
        "conv_bias": gaussian(keys[7], (LAYERS, D), 0.5, 3.0, (), jnp.float32),
    }


def rms_scale(values, gain_row):
    mean_square = lax.optimization_barrier(jnp.mean(values * values, axis=-1, keepdims=True))
    return values * lax.rsqrt(mean_square + 1e-06) * gain_row

def slot_layout(owner_list, valid_rows):
    sources = TILES // TILES_DEV
    capacity = 2 * TILES_DEV
    owner_grid = owner_list.reshape(sources, TILES_DEV)
    same_owner = owner_grid[:, :, None] == owner_grid[:, None, :]
    earlier = jnp.arange(TILES_DEV)[None, :] < jnp.arange(TILES_DEV)[:, None]
    order_in = lax.optimization_barrier(jnp.sum((same_owner & earlier[None]).astype(jnp.int32), axis=-1))
    source_ids = jnp.arange(sources, dtype=jnp.int32)[:, None]
    slot_of = (owner_grid * capacity + source_ids * SEND_MOST + order_in).reshape(TILES).astype(jnp.int32)
    slot_tile = jnp.zeros((SLOTS,), jnp.int32).at[slot_of].set(jnp.arange(TILES, dtype=jnp.int32))
    slot_rows = jnp.zeros((SLOTS,), jnp.int32).at[slot_of].set(valid_rows)
    return (slot_tile, slot_rows)

def reference(patches, owner_list, valid_rows, embed_weight, embed_bias, norm_gain, conv_kernel, conv_bias):
    capacity = 2 * TILES_DEV
    slot_tile, slot_rows = slot_layout(owner_list, valid_rows)

    def one_owner(owner_index):
        start = (owner_index * capacity).astype(jnp.int32)
        tile_ids = lax.dynamic_slice_in_dim(slot_tile, start, capacity)
        row_counts = lax.dynamic_slice_in_dim(slot_rows, start, capacity)
        chosen = jnp.take(patches, tile_ids, axis=1)
        flat_rows = chosen.reshape(FRAMES * capacity * TILE_ROWS, PF)
        hidden = jnp.dot(flat_rows, embed_weight, preferred_element_type=jnp.float32) + embed_bias
        hidden = hidden.astype(jnp.bfloat16).reshape(FRAMES, capacity, TILE_ROWS, D)
        for layer in range(LAYERS):
            framed = jnp.concatenate([jnp.zeros((2, capacity, TILE_ROWS, D), jnp.bfloat16), hidden], axis=0)
            normed = rms_scale(framed.astype(jnp.float32), norm_gain[layer])
            mixed = conv_kernel[layer, 0] * normed[2:] + conv_kernel[layer, 1] * normed[1:-1] + conv_kernel[layer, 2] * normed[:-2] + conv_bias[layer]
            hidden = (hidden.astype(jnp.float32) + jax.nn.silu(mixed)).astype(jnp.bfloat16)
        live_rows = jnp.arange(TILE_ROWS, dtype=jnp.int32)[None, :] < row_counts[:, None]
        return jnp.where(live_rows[None, :, :, None], hidden, jnp.zeros_like(hidden))
    stacked = lax.map(one_owner, jnp.arange(N_SPACE, dtype=jnp.int32))
    return jnp.transpose(stacked, (1, 0, 2, 3, 4)).reshape(FRAMES, SLOTS, TILE_ROWS, D)
```

```python
import functools

import jax
import jax.numpy as jnp
from jax import lax
from jax.experimental import pallas as pl
from jax.experimental.pallas import tpu as pltpu
from jax.sharding import Mesh, PartitionSpec as P

D = 3072
PF = 64
LAYERS = 4
F_DEV = 4
TILES_DEV = 16
TILE_ROWS = 8
SLOTS_DEV = 2 * TILES_DEV
HALO = 2 * LAYERS
FRAMES_IN = HALO + F_DEV
LANES = 128
BLOCK = 16
MAX_ROWS = SLOTS_DEV * TILE_ROWS
COPIED = SLOTS_DEV * F_DEV


def send_kernel(sources, rows_out, me_ref, owner_ref, patches_ref, out_ref):
    per_pair = SLOTS_DEV // sources
    me = me_ref[0]
    lane = lax.broadcasted_iota(jnp.int32, (1, F_DEV * TILES_DEV), 1)
    tile = lane % TILES_DEV
    owners = [owner_ref[me * TILES_DEV + k] for k in range(TILES_DEV)]
    wanted = jnp.full((1, F_DEV * TILES_DEV), -1, jnp.int32)
    for k in range(TILES_DEV):
        order = jnp.int32(0)
        for before in range(k):
            order = order + (owners[before] == owners[k]).astype(jnp.int32)
        row = owners[k] * (F_DEV * per_pair) + order
        wanted = jnp.where(tile == k, row, wanted)
    wanted = wanted + (lane // TILES_DEV) * per_pair
    place = lax.broadcasted_iota(jnp.int32, (COPIED, F_DEV * TILES_DEV), 0)
    chosen = (place == wanted).astype(jnp.bfloat16)
    sent = jnp.dot(chosen, patches_ref[...], preferred_element_type=jnp.float32)
    sent = sent.astype(jnp.bfloat16)
    for copy in range(rows_out // COPIED):
        out_ref[copy * COPIED : (copy + 1) * COPIED, :] = sent


def main_kernel(
    sources,
    at_ref,
    owner_ref,
    valid_ref,
    got_ref,
    weight_ref,
    bias_ref,
    gain_ref,
    conv_ref,
    conv_bias_ref,
    out_ref,
    rows_ref,
    base_ref,
    place_ref,
    coef_ref,
    twice_ref,
    picked_ref,
    h_ref,
    square_ref,
    scale_ref,
    staged_ref,
    sems,
):
    per_pair = SLOTS_DEV // sources
    y, c, me = at_ref[0], at_ref[1], at_ref[2]
    frame0 = (2 * y + c) * F_DEV - HALO

    def clear(s, carry):
        rows_ref[s] = 0
        return carry

    lax.fori_loop(0, SLOTS_DEV, clear, 0)

    def one_source(s, carry):
        found = jnp.int32(0)
        for k in range(TILES_DEV):
            hit = owner_ref[s * TILES_DEV + k] == me
            where = jnp.where(hit, s * per_pair + found, SLOTS_DEV)
            rows_ref[where] = valid_ref[s * TILES_DEV + k]
            found = found + hit.astype(jnp.int32)
        return carry

    lax.fori_loop(0, sources, one_source, 0)

    row_in_tile = lax.broadcasted_iota(jnp.int32, (TILE_ROWS, LANES), 0)
    lane = lax.broadcasted_iota(jnp.int32, (1, LANES), 1)
    lane_slot = (lane // (F_DEV * per_pair)) * per_pair + lane % per_pair
    lane_frame = (lane % (F_DEV * per_pair)) // per_pair
    total = jnp.int32(0)
    first = jnp.full((1, LANES), 0, jnp.int32)
    after = jnp.full((1, LANES), 0, jnp.int32)
    for s in range(SLOTS_DEV):
        rows = rows_ref[s]
        base_ref[s] = total
        place_ref[s * TILE_ROWS : (s + 1) * TILE_ROWS, :] = jnp.where(
            row_in_tile < rows, total + row_in_tile, -1
        )
        first = jnp.where(lane_slot == s, total, first)
        total = total + rows
        after = jnp.where(lane_slot == s, total, after)
    blocks = (total + BLOCK - 1) // BLOCK

    for layer in range(LAYERS):
        gain = gain_ref[layer : layer + 1, :]
        for tap in range(3):
            row = 0.5 * conv_ref[layer * 3 + tap : layer * 3 + tap + 1, :] * gain
            coef_ref[layer, tap] = jnp.broadcast_to(row, (BLOCK, D)).astype(jnp.bfloat16)
        row = 0.5 * conv_bias_ref[layer : layer + 1, :]
        coef_ref[layer, 3] = jnp.broadcast_to(row, (BLOCK, D)).astype(jnp.bfloat16)
    twice_ref[:PF, :] = weight_ref[...]
    twice_ref[PF:, :] = weight_ref[...]

    behind = (jnp.maximum(y - 1, 0), c)
    before = (jnp.where(c == 1, y, jnp.maximum(y - 1, 0)), 1 - c)
    held = (behind, before, (y, c))

    def embed(b, carry):
        line = lax.broadcasted_iota(jnp.int32, (F_DEV * BLOCK, LANES), 0)
        row = line % BLOCK + b * BLOCK
        chosen = (row >= first) & (row < after) & (line // BLOCK == lane_frame)
        in_tile = jnp.sum(jnp.where(chosen, row - first, 0).astype(jnp.float32), axis=1, keepdims=True)
        chosen = chosen.astype(jnp.bfloat16)
        part = lax.broadcasted_iota(jnp.int32, (F_DEV * BLOCK, LANES), 1) // PF
        in_tile = in_tile.astype(jnp.int32)
        for d in range(3):
            yy, cc = held[d]
            wide = jnp.dot(chosen, got_ref[cc, yy], preferred_element_type=jnp.float32)
            own = jnp.zeros((F_DEV * BLOCK, LANES), jnp.float32)
            for q in range(TILE_ROWS * PF // LANES):
                own = jnp.where(part + 2 * q == in_tile, wide[:, q * LANES : (q + 1) * LANES], own)
            picked_ref[d * F_DEV * BLOCK : (d + 1) * F_DEV * BLOCK, :] = own.astype(jnp.bfloat16)
        rows = pl.ds(pl.multiple_of(b * BLOCK, BLOCK), BLOCK)
        squares = [None] * FRAMES_IN
        for n in range(D // 256):
            at = n * 256
            value = jnp.dot(
                picked_ref[...], twice_ref[:, at : at + 256], preferred_element_type=jnp.float32
            )
            value = (value + bias_ref[:, at : at + 256]).astype(jnp.bfloat16)
            for t in range(FRAMES_IN):
                piece = value[t * BLOCK : (t + 1) * BLOCK, :]
                h_ref[t, rows, at : at + 256] = piece
                square = piece * piece
                square = square[:, :LANES] + square[:, LANES:]
                squares[t] = square if n == 0 else squares[t] + square
        for t in range(FRAMES_IN):
            square_ref[b, t * BLOCK : (t + 1) * BLOCK, :] = squares[t]
        return carry

    lax.fori_loop(0, blocks, embed, 0)

    ones = jnp.ones((LANES, LANES), jnp.bfloat16)
    for layer in range(LAYERS):
        start = 2 * layer

        def scales(b, carry, start=start):
            mean = jnp.dot(
                square_ref[b, start * BLOCK :, :], ones, preferred_element_type=jnp.float32
            )
            scale = lax.rsqrt(mean * (1.0 / D) + 1e-06)
            for t in range(start, FRAMES_IN):
                piece = scale[(t - start) * BLOCK : (t - start + 1) * BLOCK, :]
                piece = jnp.where(frame0 + t >= 0, piece, 0.0)
                scale_ref[b, t * BLOCK : (t + 1) * BLOCK, :] = piece.astype(jnp.bfloat16)
            return carry

        lax.fori_loop(0, blocks, scales, 0)

        def convolve(b, carry, layer=layer, start=start):
            rows = pl.ds(pl.multiple_of(b * BLOCK, BLOCK), BLOCK)
            scale = [
                scale_ref[b, t * BLOCK : (t + 1) * BLOCK, :] for t in range(start, FRAMES_IN)
            ]

            def chunk(n, squares):
                squares = list(squares)
                for u in range(2):
                    cols = pl.ds(pl.multiple_of(n * 256 + u * LANES, LANES), LANES)
                    k0, k1, k2, shift = (coef_ref[layer, i, :, cols] for i in range(4))
                    two_back = h_ref[start, rows, cols] * scale[0]
                    one_back = h_ref[start + 1, rows, cols] * scale[1]
                    for t in range(start + 2, FRAMES_IN):
                        value = h_ref[t, rows, cols]
                        normed = value * scale[t - start]
                        half = (k0 * normed + k1 * one_back) + (k2 * two_back + shift)
                        value = value + (half + half * jnp.tanh(half))
                        h_ref[t, rows, cols] = value
                        if layer < LAYERS - 1:
                            squares[t - start - 2] = squares[t - start - 2] + value * value
                        two_back, one_back = one_back, normed
                return tuple(squares)

            zeros = jnp.zeros((BLOCK, LANES), jnp.bfloat16)
            squares = lax.fori_loop(0, D // 256, chunk, (zeros,) * (FRAMES_IN - start - 2))
            if layer < LAYERS - 1:
                for t in range(start + 2, FRAMES_IN):
                    square_ref[b, t * BLOCK : (t + 1) * BLOCK, :] = squares[t - start - 2]
            return carry

        lax.fori_loop(0, blocks, convolve, 0)

    def wipe(b, carry):
        rows = pl.ds(pl.multiple_of(b * BLOCK, BLOCK), BLOCK)
        for t in range(HALO, FRAMES_IN):
            h_ref[t, rows, :] = jnp.zeros((BLOCK, D), jnp.bfloat16)
        return carry

    lax.fori_loop(blocks, MAX_ROWS // BLOCK, wipe, 0)

    wide_row = lax.broadcasted_iota(jnp.int32, (MAX_ROWS, LANES), 1)
    spread = jnp.concatenate(
        [(place_ref[...] == wide_row + q * LANES).astype(jnp.bfloat16) for q in range(MAX_ROWS // LANES)],
        axis=1,
    )
    for t in range(F_DEV):

        def place(n, carry, t=t):
            cols = pl.ds(pl.multiple_of(n * 256, 256), 256)
            value = jnp.dot(spread, h_ref[HALO + t, :, cols], preferred_element_type=jnp.float32)
            staged_ref[t, :, cols] = value.astype(jnp.bfloat16)
            return carry

        lax.fori_loop(0, D // 256, place, 0)
        pltpu.make_async_copy(staged_ref.at[t], out_ref.at[t], sems.at[t]).start()
    for t in range(F_DEV):
        pltpu.make_async_copy(staged_ref.at[t], out_ref.at[t], sems.at[t]).wait()


def per_device(
    patches, owner_list, valid_rows, embed_weight, embed_bias, norm_gain, conv_kernel, conv_bias
):
    sources = lax.axis_size("space")
    chips = lax.axis_size("y")
    here = jnp.stack([lax.axis_index("y"), lax.axis_index("c"), lax.axis_index("space")])
    here = here.astype(jnp.int32)
    smem = pl.BlockSpec(memory_space=pltpu.SMEM)
    vmem = pl.BlockSpec(memory_space=pltpu.VMEM)
    width = TILE_ROWS * PF
    outgoing = pl.pallas_call(
        functools.partial(send_kernel, sources, chips * COPIED),
        out_shape=jax.ShapeDtypeStruct((chips * COPIED, width), jnp.bfloat16),
        in_specs=[smem, smem, vmem],
        out_specs=vmem,
        name="send",
    )(here[2:], owner_list, patches.reshape(F_DEV * TILES_DEV, width))
    arrived = lax.all_to_all(outgoing, ("y", "space"), split_axis=0, concat_axis=0, tiled=True)
    arrived = arrived.reshape(chips, COPIED, width)
    other = lax.ppermute(arrived, "c", [(0, 1), (1, 0)])
    core = lax.axis_index("c")
    got = jnp.stack([jnp.where(core == 0, arrived, other), jnp.where(core == 0, other, arrived)])
    packed = pl.pallas_call(
        functools.partial(main_kernel, sources),
        out_shape=jax.ShapeDtypeStruct((F_DEV, MAX_ROWS, D), jnp.bfloat16),
        in_specs=[smem, smem, smem] + [vmem] * 6,
        out_specs=pl.BlockSpec(memory_space=pl.ANY),
        scratch_shapes=[
            pltpu.SMEM((SLOTS_DEV + 1,), jnp.int32),
            pltpu.SMEM((SLOTS_DEV + 1,), jnp.int32),
            pltpu.VMEM((MAX_ROWS, LANES), jnp.int32),
            pltpu.VMEM((LAYERS, 4, BLOCK, D), jnp.bfloat16),
            pltpu.VMEM((2 * PF, D), jnp.bfloat16),
            pltpu.VMEM((FRAMES_IN * BLOCK, LANES), jnp.bfloat16),
            pltpu.VMEM((FRAMES_IN, MAX_ROWS, D), jnp.bfloat16),
            pltpu.VMEM((MAX_ROWS // BLOCK, FRAMES_IN * BLOCK, LANES), jnp.bfloat16),
            pltpu.VMEM((MAX_ROWS // BLOCK, FRAMES_IN * BLOCK, LANES), jnp.bfloat16),
            pltpu.VMEM((F_DEV, MAX_ROWS, D), jnp.bfloat16),
            pltpu.SemaphoreType.DMA((F_DEV,)),
        ],
        compiler_params=pltpu.CompilerParams(vmem_limit_bytes=48 << 20),
        name="layers",
    )(
        here,
        owner_list,
        valid_rows,
        got,
        embed_weight,
        embed_bias.reshape(1, D),
        norm_gain,
        conv_kernel.reshape(LAYERS * 3, D),
        conv_bias,
    )
    return packed.reshape(F_DEV, SLOTS_DEV, TILE_ROWS, D)


def solution(mesh):
    frames, space = mesh.shape["tm"], mesh.shape["space"]
    split = Mesh(mesh.devices.reshape(frames // 2, 2, space), ("y", "c", "space"))
    placed = (P(("y", "c"), "space", None), P(), P(), P(), P(), P(), P(), P())
    return jax.shard_map(
        per_device,
        mesh=split,
        in_specs=placed,
        out_specs=P(("y", "c"), "space", None, None),
        check_vma=False,
    )
```

```python
import functools

import jax
import jax.numpy as jnp
from jax import lax
from jax.experimental import pallas as pl
from jax.experimental.pallas import tpu as pltpu
from jax.sharding import Mesh, PartitionSpec as P

D = 3072
PF = 64
LAYERS = 4
F_DEV = 4
TILES_DEV = 16
TILE_ROWS = 8
SLOTS_DEV = 2 * TILES_DEV
HALO = 2 * LAYERS
FRAMES_IN = HALO + F_DEV
LANES = 128
BLOCK = 8
GROUP = 32
TOGETHER = 8
VMEM_LIMIT = 58 << 20
MAX_ROWS = SLOTS_DEV * TILE_ROWS
COPIED = SLOTS_DEV * F_DEV


def send_kernel(sources, rows_out, me_ref, owner_ref, patches_ref, out_ref):
    per_pair = SLOTS_DEV // sources
    me = me_ref[0]
    lane = lax.broadcasted_iota(jnp.int32, (1, F_DEV * TILES_DEV), 1)
    tile = lane % TILES_DEV
    owners = [owner_ref[me * TILES_DEV + k] for k in range(TILES_DEV)]
    wanted = jnp.full((1, F_DEV * TILES_DEV), -1, jnp.int32)
    for k in range(TILES_DEV):
        order = jnp.int32(0)
        for before in range(k):
            order = order + (owners[before] == owners[k]).astype(jnp.int32)
        row = owners[k] * (F_DEV * per_pair) + order
        wanted = jnp.where(tile == k, row, wanted)
    wanted = wanted + (lane // TILES_DEV) * per_pair
    place = lax.broadcasted_iota(jnp.int32, (COPIED, F_DEV * TILES_DEV), 0)
    chosen = (place == wanted).astype(jnp.bfloat16)
    sent = jnp.dot(chosen, patches_ref[...], preferred_element_type=jnp.float32)
    sent = sent.astype(jnp.bfloat16)
    for copy in range(rows_out // COPIED):
        out_ref[copy * COPIED : (copy + 1) * COPIED, :] = sent


def main_kernel(
    sources,
    at_ref,
    owner_ref,
    valid_ref,
    arrived_ref,
    other_ref,
    weight_ref,
    bias_ref,
    gain_ref,
    conv_ref,
    conv_bias_ref,
    out_ref,
    rows_ref,
    base_ref,
    got_ref,
    twice_ref,
    bias_row_ref,
    gain_row_ref,
    conv_row_ref,
    conv_bias_row_ref,
    coef_ref,
    picked_ref,
    h_ref,
    square_ref,
    scale_ref,
    staged_ref,
    in_sems,
    out_sems,
):
    per_pair = SLOTS_DEV // sources
    y, c, me = at_ref[0], at_ref[1], at_ref[2]
    frame0 = (2 * y + c) * F_DEV - HALO
    loads = [
        pltpu.make_async_copy(source, target, in_sems.at[i])
        for i, (source, target) in enumerate(
            [
                (gain_ref, gain_row_ref),
                (conv_ref, conv_row_ref),
                (conv_bias_ref, conv_bias_row_ref),
                (bias_ref, bias_row_ref),
                (weight_ref, twice_ref.at[:PF]),
                (weight_ref, twice_ref.at[PF:]),
                (arrived_ref, got_ref.at[0]),
                (other_ref, got_ref.at[1]),
            ]
        )
    ]
    for load in loads:
        load.start()

    def clear(s, carry):
        rows_ref[s] = 0
        return carry

    lax.fori_loop(0, SLOTS_DEV, clear, 0)

    def one_source(s, carry):
        found = jnp.int32(0)
        for k in range(TILES_DEV):
            hit = owner_ref[s * TILES_DEV + k] == me
            where = jnp.where(hit, s * per_pair + found, SLOTS_DEV)
            rows_ref[where] = valid_ref[s * TILES_DEV + k]
            found = found + hit.astype(jnp.int32)
        return carry

    lax.fori_loop(0, sources, one_source, 0)

    lane = lax.broadcasted_iota(jnp.int32, (1, LANES), 1)
    lane_slot = (lane // (F_DEV * per_pair)) * per_pair + lane % per_pair
    lane_frame = (lane % (F_DEV * per_pair)) // per_pair
    total = jnp.int32(0)
    first = jnp.full((1, LANES), 0, jnp.int32)
    after = jnp.full((1, LANES), 0, jnp.int32)
    for s in range(SLOTS_DEV):
        base_ref[s] = total
        first = jnp.where(lane_slot == s, total, first)
        total = total + rows_ref[s]
        after = jnp.where(lane_slot == s, total, after)
    blocks = (total + BLOCK - 1) // BLOCK
    groups = (total + GROUP - 1) // GROUP

    for load in loads[:3]:
        load.wait()
    for layer in range(LAYERS):
        gain = gain_row_ref[layer : layer + 1, :]
        for tap in range(3):
            row = conv_row_ref[layer * 3 + tap : layer * 3 + tap + 1, :] * gain
            coef_ref[layer, tap] = jnp.broadcast_to(row, (BLOCK, D))
        row = conv_bias_row_ref[layer : layer + 1, :]
        coef_ref[layer, 3] = jnp.broadcast_to(row, (BLOCK, D))
    for load in loads[3:]:
        load.wait()

    held = (
        (0, jnp.maximum(y - 1, 0)),
        (1, jnp.where(c == 1, y, jnp.maximum(y - 1, 0))),
        (0, y),
    )

    def embed(g, carry):
        lines = F_DEV * GROUP
        line = lax.broadcasted_iota(jnp.int32, (lines, LANES), 0)
        row = line % GROUP + g * GROUP
        chosen = (row >= first) & (row < after) & (line // GROUP == lane_frame)
        in_tile = jnp.sum(jnp.where(chosen, row - first, 0).astype(jnp.float32), axis=1, keepdims=True)
        in_tile = in_tile.astype(jnp.int32)
        chosen = chosen.astype(jnp.bfloat16)
        part = lax.broadcasted_iota(jnp.int32, (lines, LANES), 1) // PF
        for d in range(3):
            array, chip = held[d]
            wide = jnp.dot(chosen, got_ref[array, chip], preferred_element_type=jnp.float32)
            own = jnp.zeros((lines, LANES), jnp.float32)
            for q in range(TILE_ROWS * PF // LANES):
                own = jnp.where(part + 2 * q == in_tile, wide[:, q * LANES : (q + 1) * LANES], own)
            picked_ref[d * lines : (d + 1) * lines, :] = own.astype(jnp.bfloat16)
        for n in range(D // 256):
            at = n * 256
            value = jnp.dot(
                picked_ref[...], twice_ref[:, at : at + 256], preferred_element_type=jnp.float32
            )
            value = value + bias_row_ref[:, at : at + 256]
            for t in range(FRAMES_IN):
                for i in range(GROUP // BLOCK):
                    b = g * (GROUP // BLOCK) + i
                    piece = value[t * GROUP + i * BLOCK : t * GROUP + (i + 1) * BLOCK, :]
                    h_ref[b, t, :, at : at + 256] = piece
                    square = piece * piece
                    square = square[:, :LANES] + square[:, LANES:]
                    if n == 0:
                        square_ref[b, t] = square
                    else:
                        square_ref[b, t] += square
        return carry

    lax.fori_loop(0, groups, embed, 0)

    ones = jnp.ones((LANES, LANES), jnp.bfloat16)
    for layer in range(LAYERS):
        start = 2 * layer

        def scales(g, carry, start=start):
            count = FRAMES_IN - start
            squares = square_ref[pl.ds(g * TOGETHER, TOGETHER), start:].reshape(TOGETHER * count * BLOCK, LANES)
            mean = jnp.dot(squares.astype(jnp.bfloat16), ones, preferred_element_type=jnp.float32)
            scale = lax.rsqrt(mean * (1.0 / D) + 1e-06).reshape(TOGETHER, count, BLOCK, LANES)
            for t in range(start, FRAMES_IN):
                piece = jnp.where(frame0 + t >= 0, scale[:, t - start], 0.0)
                scale_ref[pl.ds(g * TOGETHER, TOGETHER), t] = piece
            return carry

        lax.fori_loop(0, (blocks + TOGETHER - 1) // TOGETHER, scales, 0)

        def convolve(b, carry, layer=layer, start=start):
            scale = [scale_ref[b, t] for t in range(start, FRAMES_IN)]

            zeros = jnp.zeros((BLOCK, LANES), jnp.float32)
            squares = [zeros] * (FRAMES_IN - start - 2)
            for n in range(D // LANES):
                cols = slice(n * LANES, (n + 1) * LANES)
                k0, k1, k2, shift = (coef_ref[layer, i, :, cols] for i in range(4))
                two_back = h_ref[b, start, :, cols] * scale[0]
                one_back = h_ref[b, start + 1, :, cols] * scale[1]
                for t in range(start + 2, FRAMES_IN):
                    value = h_ref[b, t, :, cols]
                    normed = value * scale[t - start]
                    mixed = (k0 * normed + k1 * one_back) + (k2 * two_back + shift)
                    value = value + mixed * jax.nn.sigmoid(mixed)
                    h_ref[b, t, :, cols] = value
                    if layer < LAYERS - 1:
                        squares[t - start - 2] = squares[t - start - 2] + value * value
                    two_back, one_back = one_back, normed
            if layer < LAYERS - 1:
                for t in range(start + 2, FRAMES_IN):
                    square_ref[b, t] = squares[t - start - 2]
            return carry

        lax.fori_loop(0, blocks, convolve, 0)

    def place(s, carry):
        base = base_ref[s]
        offset = base % BLOCK
        b = base // BLOCK
        live = lax.broadcasted_iota(jnp.int32, (TILE_ROWS, D), 0) < rows_ref[s]
        for t in range(F_DEV):
            value = jnp.concatenate([h_ref[b, HALO + t], h_ref[b + 1, HALO + t]], axis=0)
            value = pltpu.roll(value, (2 * BLOCK - offset) % (2 * BLOCK), 0)
            value = jnp.where(live, value[:TILE_ROWS, :], 0.0)
            staged_ref[t, s] = value.astype(jnp.bfloat16)
        pltpu.make_async_copy(staged_ref.at[:, s], out_ref.at[:, s], out_sems.at[s]).start()
        return carry

    lax.fori_loop(0, SLOTS_DEV, place, 0)

    def finish(s, carry):
        pltpu.make_async_copy(staged_ref.at[:, s], out_ref.at[:, s], out_sems.at[s]).wait()
        return carry

    lax.fori_loop(0, SLOTS_DEV, finish, 0)


def main_call(sources, chips):
    smem = pl.BlockSpec(memory_space=pltpu.SMEM)
    hbm = pl.BlockSpec(memory_space=pl.ANY)
    return pl.pallas_call(
        functools.partial(main_kernel, sources),
        out_shape=jax.ShapeDtypeStruct((F_DEV, SLOTS_DEV, TILE_ROWS, D), jnp.bfloat16),
        in_specs=[smem, smem, smem] + [hbm] * 7,
        out_specs=hbm,
        scratch_shapes=[
            pltpu.SMEM((SLOTS_DEV + 1,), jnp.int32),
            pltpu.SMEM((SLOTS_DEV + 1,), jnp.int32),
            pltpu.VMEM((2, chips, COPIED, TILE_ROWS * PF), jnp.bfloat16),
            pltpu.VMEM((2 * PF, D), jnp.bfloat16),
            pltpu.VMEM((1, D), jnp.float32),
            pltpu.VMEM((LAYERS, D), jnp.float32),
            pltpu.VMEM((LAYERS * 3, D), jnp.float32),
            pltpu.VMEM((LAYERS, D), jnp.float32),
            pltpu.VMEM((LAYERS, 4, BLOCK, D), jnp.float32),
            pltpu.VMEM((FRAMES_IN * GROUP, LANES), jnp.bfloat16),
            pltpu.VMEM((MAX_ROWS // BLOCK + 1, FRAMES_IN, BLOCK, D), jnp.float32),
            pltpu.VMEM((MAX_ROWS // BLOCK, FRAMES_IN, BLOCK, LANES), jnp.float32),
            pltpu.VMEM((MAX_ROWS // BLOCK, FRAMES_IN, BLOCK, LANES), jnp.float32),
            pltpu.VMEM((F_DEV, SLOTS_DEV, TILE_ROWS, D), jnp.bfloat16),
            pltpu.SemaphoreType.DMA((8,)),
            pltpu.SemaphoreType.DMA((SLOTS_DEV,)),
        ],
        compiler_params=pltpu.CompilerParams(vmem_limit_bytes=VMEM_LIMIT),
        name="layers",
    )


def per_device(
    patches, owner_list, valid_rows, embed_weight, embed_bias, norm_gain, conv_kernel, conv_bias
):
    sources = lax.axis_size("space")
    chips = lax.axis_size("y")
    here = jnp.stack([lax.axis_index("y"), lax.axis_index("c"), lax.axis_index("space")])
    here = here.astype(jnp.int32)
    smem = pl.BlockSpec(memory_space=pltpu.SMEM)
    vmem = pl.BlockSpec(memory_space=pltpu.VMEM)
    width = TILE_ROWS * PF
    outgoing = pl.pallas_call(
        functools.partial(send_kernel, sources, chips * COPIED),
        out_shape=jax.ShapeDtypeStruct((chips * COPIED, width), jnp.bfloat16),
        in_specs=[smem, smem, vmem],
        out_specs=vmem,
        name="send",
    )(here[2:], owner_list, patches.reshape(F_DEV * TILES_DEV, width))
    arrived = lax.all_to_all(outgoing, ("y", "space"), split_axis=0, concat_axis=0, tiled=True)
    arrived = arrived.reshape(chips, COPIED, width)
    other = lax.ppermute(arrived, "c", [(0, 1), (1, 0)])
    return main_call(sources, chips)(
        here,
        owner_list,
        valid_rows,
        arrived,
        other,
        embed_weight,
        embed_bias.reshape(1, D),
        norm_gain,
        conv_kernel.reshape(LAYERS * 3, D),
        conv_bias,
    )


def solution(mesh):
    frames, space = mesh.shape["tm"], mesh.shape["space"]
    split = Mesh(mesh.devices.reshape(frames // 2, 2, space), ("y", "c", "space"))
    placed = (P(("y", "c"), "space", None), P(), P(), P(), P(), P(), P(), P())
    return jax.shard_map(
        per_device,
        mesh=split,
        in_specs=placed,
        out_specs=P(("y", "c"), "space", None, None),
        check_vma=False,
    )
```

```python
import functools

import jax
import jax.numpy as jnp
from jax import lax
from jax.experimental import pallas as pl
from jax.experimental.pallas import tpu as pltpu
from jax.sharding import Mesh, PartitionSpec as P

D = 3072
PF = 64
LAYERS = 4
F_DEV = 4
TILES_DEV = 16
TILE_ROWS = 8
SLOTS_DEV = 2 * TILES_DEV
HALO = 2 * LAYERS
FRAMES_IN = HALO + F_DEV
LANES = 128
BLOCK = 8
GROUP = 32
WIDE = 256
TOGETHER = 8
VMEM_LIMIT = 54 << 20
MAX_ROWS = SLOTS_DEV * TILE_ROWS
COPIED = SLOTS_DEV * F_DEV


def send_kernel(sources, rows_out, owner_ref, patches_ref, out_ref):
    per_pair = SLOTS_DEV // sources
    me = lax.axis_index("space")
    lane = lax.broadcasted_iota(jnp.int32, (1, F_DEV * TILES_DEV), 1)
    tile = lane % TILES_DEV
    owners = [owner_ref[me * TILES_DEV + k] for k in range(TILES_DEV)]
    wanted = jnp.full((1, F_DEV * TILES_DEV), -1, jnp.int32)
    for k in range(TILES_DEV):
        order = jnp.int32(0)
        for before in range(k):
            order = order + (owners[before] == owners[k]).astype(jnp.int32)
        row = owners[k] * (F_DEV * per_pair) + order
        wanted = jnp.where(tile == k, row, wanted)
    wanted = wanted + (lane // TILES_DEV) * per_pair
    place = lax.broadcasted_iota(jnp.int32, (COPIED, F_DEV * TILES_DEV), 0)
    chosen = (place == wanted).astype(jnp.bfloat16)
    sent = jnp.dot(chosen, patches_ref[...], preferred_element_type=jnp.float32)
    sent = sent.astype(jnp.bfloat16)
    for copy in range(rows_out // COPIED):
        out_ref[copy * COPIED : (copy + 1) * COPIED, :] = sent


def main_kernel(
    sources,
    owner_ref,
    valid_ref,
    arrived_ref,
    other_ref,
    weight_ref,
    bias_ref,
    gain_ref,
    conv_ref,
    conv_bias_ref,
    out_ref,
    rows_ref,
    base_ref,
    ready_ref,
    got_ref,
    twice_ref,
    bias_row_ref,
    gain_row_ref,
    conv_row_ref,
    conv_bias_row_ref,
    coef_ref,
    picked_ref,
    h_ref,
    square_ref,
    scale_ref,
    staged_ref,
    in_sems,
    out_sems,
):
    per_pair = SLOTS_DEV // sources
    y, c, me = (lax.axis_index(name) for name in ("y", "c", "space"))
    frame0 = (2 * y + c) * F_DEV - HALO
    loads = [
        pltpu.make_async_copy(source, target, in_sems.at[i])
        for i, (source, target) in enumerate(
            [
                (weight_ref, twice_ref.at[:PF]),
                (arrived_ref, got_ref.at[0]),
                (other_ref, got_ref.at[1]),
                (bias_ref, bias_row_ref),
                (conv_ref, conv_row_ref),
                (gain_ref, gain_row_ref),
                (conv_bias_ref, conv_bias_row_ref),
            ]
        )
    ]
    for load in loads:
        load.start()

    def clear(s, carry):
        rows_ref[s] = 0
        return carry

    lax.fori_loop(0, SLOTS_DEV, clear, 0)

    def one_source(s, carry):
        found = jnp.int32(0)
        for k in range(TILES_DEV):
            hit = owner_ref[s * TILES_DEV + k] == me
            where = jnp.where(hit, s * per_pair + found, SLOTS_DEV)
            rows_ref[where] = valid_ref[s * TILES_DEV + k]
            found = found + hit.astype(jnp.int32)
        return carry

    lax.fori_loop(0, sources, one_source, 0)

    lane = lax.broadcasted_iota(jnp.int32, (1, LANES), 1)
    lane_slot = (lane // (F_DEV * per_pair)) * per_pair + lane % per_pair
    lane_frame = (lane % (F_DEV * per_pair)) // per_pair
    total = jnp.int32(0)
    first = jnp.full((1, LANES), 0, jnp.int32)
    after = jnp.full((1, LANES), 0, jnp.int32)
    for s in range(SLOTS_DEV):
        base_ref[s] = total
        first = jnp.where(lane_slot == s, total, first)
        total = total + rows_ref[s]
        after = jnp.where(lane_slot == s, total, after)
        ready_ref[jnp.maximum(total - 1, 0) // BLOCK] = s + 1
    blocks = (total + BLOCK - 1) // BLOCK
    groups = (total + GROUP - 1) // GROUP

    for load in loads[:4]:
        load.wait()
    twice_ref[PF:, :] = twice_ref[:PF, :]

    held = (
        (got_ref.at[0], jnp.maximum(y - 1, 0)),
        (got_ref.at[1], jnp.where(c == 1, y, jnp.maximum(y - 1, 0))),
        (got_ref.at[0], y),
    )

    def embed(g, carry):
        lines = F_DEV * GROUP
        line = lax.broadcasted_iota(jnp.int32, (lines, LANES), 0)
        row = line % GROUP + g * GROUP
        chosen = (row >= first) & (row < after) & (line // GROUP == lane_frame)
        in_tile = jnp.sum(jnp.where(chosen, row - first, 0).astype(jnp.float32), axis=1, keepdims=True)
        in_tile = in_tile.astype(jnp.int32)
        chosen = chosen.astype(jnp.bfloat16)
        part = lax.broadcasted_iota(jnp.int32, (lines, LANES), 1) // PF
        for d in range(3):
            array, chip = held[d]
            wide = jnp.dot(chosen, array[chip], preferred_element_type=jnp.float32)
            own = jnp.zeros((lines, LANES), jnp.float32)
            for q in range(TILE_ROWS * PF // LANES):
                own = jnp.where(part + 2 * q == in_tile, wide[:, q * LANES : (q + 1) * LANES], own)
            picked_ref[d * lines : (d + 1) * lines, :] = own.astype(jnp.bfloat16)
        for n in range(D // WIDE):
            at = n * WIDE
            value = jnp.dot(
                picked_ref[...], twice_ref[:, at : at + WIDE], preferred_element_type=jnp.float32
            )
            value = value + bias_row_ref[:, at : at + WIDE]
            for t in range(FRAMES_IN):
                for i in range(GROUP // BLOCK):
                    b = g * (GROUP // BLOCK) + i
                    piece = value[t * GROUP + i * BLOCK : t * GROUP + (i + 1) * BLOCK, :]
                    h_ref[b, t, :, at : at + WIDE] = piece
                    square = piece * piece
                    square = sum(square[:, k : k + LANES] for k in range(0, WIDE, LANES))
                    if n == 0:
                        square_ref[b, t] = square
                    else:
                        square_ref[b, t] += square
        return carry

    lax.fori_loop(0, groups, embed, 0)

    def place(s, carry):
        base = base_ref[s]
        offset = base % BLOCK
        b = base // BLOCK
        row = lax.broadcasted_iota(jnp.int32, (TILE_ROWS, D), 0)
        for t in range(F_DEV):
            value = jnp.where(row >= offset, h_ref[b, HALO + t], h_ref[b + 1, HALO + t])
            value = pltpu.roll(value, (BLOCK - offset) % BLOCK, 0)
            value = jnp.where(row < rows_ref[s], value, 0.0)
            staged_ref[t, s] = value.astype(jnp.bfloat16)
        pltpu.make_async_copy(staged_ref.at[:, s], out_ref.at[:, s], out_sems.at[s]).start()
        return s + 1

    for load in loads[4:]:
        load.wait()
    for layer in range(LAYERS):
        gain = gain_row_ref[layer : layer + 1, :]
        for tap in range(3):
            row = conv_row_ref[tap, layer : layer + 1, :] * gain
            coef_ref[layer, tap] = jnp.broadcast_to(row, (BLOCK, D))
        row = conv_bias_row_ref[layer : layer + 1, :]
        coef_ref[layer, 3] = jnp.broadcast_to(row, (BLOCK, D))

    ones = jnp.ones((LANES, LANES), jnp.bfloat16)
    for layer in range(LAYERS):
        start = 2 * layer

        def scales(g, carry, start=start):
            count = FRAMES_IN - start
            squares = square_ref[pl.ds(g * TOGETHER, TOGETHER), start:].reshape(TOGETHER * count * BLOCK, LANES)
            mean = jnp.dot(squares.astype(jnp.bfloat16), ones, preferred_element_type=jnp.float32)
            scale = lax.rsqrt(mean * (1.0 / D) + 1e-06).reshape(TOGETHER, count, BLOCK, LANES)
            for t in range(start, FRAMES_IN):
                piece = jnp.where(frame0 + t >= 0, scale[:, t - start], 0.0)
                scale_ref[pl.ds(g * TOGETHER, TOGETHER), t] = piece
            return carry

        lax.fori_loop(0, (blocks + TOGETHER - 1) // TOGETHER, scales, 0)

        def convolve(b, done, layer=layer, start=start):
            scale = [scale_ref[b, t] for t in range(start, FRAMES_IN)]

            zeros = jnp.zeros((BLOCK, LANES), jnp.float32)
            squares = [zeros] * (FRAMES_IN - start - 2)
            for n in range(D // LANES):
                cols = slice(n * LANES, (n + 1) * LANES)
                k0, k1, k2, shift = (coef_ref[layer, i, :, cols] for i in range(4))
                two_back = h_ref[b, start, :, cols] * scale[0]
                one_back = h_ref[b, start + 1, :, cols] * scale[1]
                for t in range(start + 2, FRAMES_IN):
                    value = h_ref[b, t, :, cols]
                    normed = value * scale[t - start]
                    mixed = (k0 * normed + k1 * one_back) + (k2 * two_back + shift)
                    value = value + mixed * jax.nn.sigmoid(mixed)
                    h_ref[b, t, :, cols] = value
                    if layer < LAYERS - 1:
                        squares[t - start - 2] = squares[t - start - 2] + value * value
                    two_back, one_back = one_back, normed
            if layer < LAYERS - 1:
                for t in range(start + 2, FRAMES_IN):
                    square_ref[b, t] = squares[t - start - 2]
                return done
            return done

        placed = jnp.int32(0)
        placed = lax.fori_loop(0, blocks, convolve, jnp.int32(0))

    lax.fori_loop(placed, SLOTS_DEV, place, placed)

    def finish(s, carry):
        pltpu.make_async_copy(staged_ref.at[:, s], out_ref.at[:, s], out_sems.at[s]).wait()
        return carry

    lax.fori_loop(0, SLOTS_DEV, finish, 0)


def main_call(sources, chips):
    smem = pl.BlockSpec(memory_space=pltpu.SMEM)
    hbm = pl.BlockSpec(memory_space=pl.ANY)
    vmem = pl.BlockSpec(memory_space=pltpu.VMEM)
    return pl.pallas_call(
        functools.partial(main_kernel, sources),
        out_shape=jax.ShapeDtypeStruct((F_DEV, SLOTS_DEV, TILE_ROWS, D), jnp.bfloat16),
        in_specs=[smem] * 2 + [hbm] * 7,
        out_specs=hbm,
        scratch_shapes=[
            pltpu.SMEM((SLOTS_DEV + 1,), jnp.int32),
            pltpu.SMEM((SLOTS_DEV + 1,), jnp.int32),
            pltpu.SMEM((MAX_ROWS // BLOCK + 1,), jnp.int32),
            pltpu.VMEM((2, chips, COPIED, TILE_ROWS * PF), jnp.bfloat16),
            pltpu.VMEM((2 * PF, D), jnp.bfloat16),
            pltpu.VMEM((1, D), jnp.float32),
            pltpu.VMEM((LAYERS, D), jnp.float32),
            pltpu.VMEM((3, LAYERS, D), jnp.float32),
            pltpu.VMEM((LAYERS, D), jnp.float32),
            pltpu.VMEM((LAYERS, 4, BLOCK, D), jnp.float32),
            pltpu.VMEM((FRAMES_IN * GROUP, LANES), jnp.bfloat16),
            pltpu.VMEM((MAX_ROWS // BLOCK + 1, FRAMES_IN, BLOCK, D), jnp.float32),
            pltpu.VMEM((MAX_ROWS // BLOCK, FRAMES_IN, BLOCK, LANES), jnp.float32),
            pltpu.VMEM((MAX_ROWS // BLOCK, FRAMES_IN, BLOCK, LANES), jnp.float32),
            pltpu.VMEM((F_DEV, SLOTS_DEV, TILE_ROWS, D), jnp.bfloat16),
            pltpu.SemaphoreType.DMA((7,)),
            pltpu.SemaphoreType.DMA((SLOTS_DEV,)),
        ],
        compiler_params=pltpu.CompilerParams(vmem_limit_bytes=VMEM_LIMIT),
        name="layers",
    )


def per_device(
    patches, owner_list, valid_rows, embed_weight, embed_bias, norm_gain, conv_kernel, conv_bias
):
    sources = lax.axis_size("space")
    chips = lax.axis_size("y")
    smem = pl.BlockSpec(memory_space=pltpu.SMEM)
    vmem = pl.BlockSpec(memory_space=pltpu.VMEM)
    width = TILE_ROWS * PF
    outgoing = pl.pallas_call(
        functools.partial(send_kernel, sources, chips * COPIED),
        out_shape=jax.ShapeDtypeStruct((chips * COPIED, width), jnp.bfloat16),
        in_specs=[smem, vmem],
        out_specs=vmem,
        name="send",
    )(owner_list, patches.reshape(F_DEV * TILES_DEV, width))
    arrived = lax.all_to_all(outgoing, ("y", "space"), split_axis=0, concat_axis=0, tiled=True)
    arrived = arrived.reshape(chips, COPIED, width)
    other = lax.ppermute(arrived, "c", [(0, 1), (1, 0)])
    return main_call(sources, chips)(
        owner_list,
        valid_rows,
        arrived,
        other,
        embed_weight,
        embed_bias.reshape(1, D),
        norm_gain,
        jnp.transpose(conv_kernel, (1, 0, 2)),
        conv_bias,
    )


def solution(mesh):
    frames, space = mesh.shape["tm"], mesh.shape["space"]
    split = Mesh(mesh.devices.reshape(frames // 2, 2, space), ("y", "c", "space"))
    placed = (P(("y", "c"), "space", None), P(), P(), P(), P(), P(), P(), P())
    return jax.shard_map(
        per_device,
        mesh=split,
        in_specs=placed,
        out_specs=P(("y", "c"), "space", None, None),
        check_vma=False,
    )
```

```python
import functools

import jax
import jax.numpy as jnp
from jax import lax
from jax.experimental import pallas as pl
from jax.experimental.pallas import tpu as pltpu
from jax.sharding import Mesh, PartitionSpec as P

D = 3072
PF = 64
LAYERS = 4
F_DEV = 4
TILES_DEV = 16
TILE_ROWS = 8
SLOTS_DEV = 2 * TILES_DEV
HALO = 2 * LAYERS
FRAMES_IN = HALO + F_DEV
LANES = 128
BLOCK = 8
GROUP = 32
TOGETHER = 24
WIDE = 256
VMEM_LIMIT = 54 << 20
MAX_ROWS = SLOTS_DEV * TILE_ROWS
COPIED = SLOTS_DEV * F_DEV


def send_kernel(sources, rows_out, owner_ref, patches_ref, out_ref):
    per_pair = SLOTS_DEV // sources
    me = lax.axis_index("space")
    lane = lax.broadcasted_iota(jnp.int32, (1, F_DEV * TILES_DEV), 1)
    tile = lane % TILES_DEV
    owners = [owner_ref[me * TILES_DEV + k] for k in range(TILES_DEV)]
    wanted = jnp.full((1, F_DEV * TILES_DEV), -1, jnp.int32)
    for k in range(TILES_DEV):
        order = jnp.int32(0)
        for before in range(k):
            order = order + (owners[before] == owners[k]).astype(jnp.int32)
        row = owners[k] * (F_DEV * per_pair) + order
        wanted = jnp.where(tile == k, row, wanted)
    wanted = wanted + (lane // TILES_DEV) * per_pair
    place = lax.broadcasted_iota(jnp.int32, (COPIED, F_DEV * TILES_DEV), 0)
    chosen = (place == wanted).astype(jnp.bfloat16)
    sent = jnp.dot(chosen, patches_ref[...], preferred_element_type=jnp.float32)
    sent = sent.astype(jnp.bfloat16)
    for copy in range(rows_out // COPIED):
        out_ref[copy * COPIED : (copy + 1) * COPIED, :] = sent


def main_kernel(
    sources,
    owner_ref,
    valid_ref,
    arrived_ref,
    other_ref,
    weight_ref,
    bias_ref,
    gain_ref,
    conv_ref,
    conv_bias_ref,
    out_ref,
    rows_ref,
    base_ref,
    got_ref,
    twice_ref,
    bias_row_ref,
    gain_row_ref,
    conv_row_ref,
    conv_bias_row_ref,
    coef_ref,
    picked_ref,
    h_ref,
    square_ref,
    scale_ref,
    staged_ref,
    in_sems,
    out_sems,
):
    per_pair = SLOTS_DEV // sources
    y, c, me = (lax.axis_index(name) for name in ("y", "c", "space"))
    frame0 = (2 * y + c) * F_DEV - HALO
    loads = [
        pltpu.make_async_copy(source, target, in_sems.at[i])
        for i, (source, target) in enumerate(
            [
                (weight_ref, twice_ref.at[:PF]),
                (arrived_ref, got_ref.at[0]),
                (other_ref, got_ref.at[1]),
                (bias_ref, bias_row_ref),
                (conv_ref, conv_row_ref),
                (gain_ref, gain_row_ref),
                (conv_bias_ref, conv_bias_row_ref),
            ]
        )
    ]
    for load in loads:
        load.start()

    def clear(s, carry):
        rows_ref[s] = 0
        return carry

    lax.fori_loop(0, SLOTS_DEV, clear, 0)

    def one_source(s, carry):
        found = jnp.int32(0)
        for k in range(TILES_DEV):
            hit = owner_ref[s * TILES_DEV + k] == me
            where = jnp.where(hit, s * per_pair + found, SLOTS_DEV)
            rows_ref[where] = valid_ref[s * TILES_DEV + k]
            found = found + hit.astype(jnp.int32)
        return carry

    lax.fori_loop(0, sources, one_source, 0)

    lane = lax.broadcasted_iota(jnp.int32, (1, LANES), 1)
    lane_slot = (lane // (F_DEV * per_pair)) * per_pair + lane % per_pair
    lane_frame = (lane % (F_DEV * per_pair)) // per_pair
    total = jnp.int32(0)
    first = jnp.full((1, LANES), 0, jnp.int32)
    after = jnp.full((1, LANES), 0, jnp.int32)
    for s in range(SLOTS_DEV):
        base_ref[s] = total
        first = jnp.where(lane_slot == s, total, first)
        total = total + rows_ref[s]
        after = jnp.where(lane_slot == s, total, after)
    blocks = (total + BLOCK - 1) // BLOCK
    groups = (total + GROUP - 1) // GROUP

    for load in loads[:4]:
        load.wait()
    twice_ref[PF:, :] = twice_ref[:PF, :]

    held = (
        (got_ref.at[0], jnp.maximum(y - 1, 0)),
        (got_ref.at[1], jnp.where(c == 1, y, jnp.maximum(y - 1, 0))),
        (got_ref.at[0], y),
    )

    def embed(g, carry):
        lines = F_DEV * GROUP
        line = lax.broadcasted_iota(jnp.int32, (lines, LANES), 0)
        row = line % GROUP + g * GROUP
        chosen = (row >= first) & (row < after) & (line // GROUP == lane_frame)
        in_tile = jnp.sum(jnp.where(chosen, row - first, 0).astype(jnp.float32), axis=1, keepdims=True)
        in_tile = in_tile.astype(jnp.int32)
        chosen = chosen.astype(jnp.bfloat16)
        part = lax.broadcasted_iota(jnp.int32, (lines, LANES), 1) // PF
        for d in range(3):
            array, chip = held[d]
            wide = jnp.dot(chosen, array[chip], preferred_element_type=jnp.float32)
            own = jnp.zeros((lines, LANES), jnp.float32)
            for q in range(TILE_ROWS * PF // LANES):
                own = jnp.where(part + 2 * q == in_tile, wide[:, q * LANES : (q + 1) * LANES], own)
            picked_ref[d * lines : (d + 1) * lines, :] = own.astype(jnp.bfloat16)
        for n in range(D // WIDE):
            at = n * WIDE
            value = jnp.dot(
                picked_ref[...], twice_ref[:, at : at + WIDE], preferred_element_type=jnp.float32
            )
            value = value + bias_row_ref[:, at : at + WIDE]
            for t in range(FRAMES_IN):
                for i in range(GROUP // BLOCK):
                    b = g * (GROUP // BLOCK) + i
                    piece = value[t * GROUP + i * BLOCK : t * GROUP + (i + 1) * BLOCK, :]
                    h_ref[b, t, :, at : at + WIDE] = piece
                    square = piece * piece
                    square = sum(square[:, k : k + LANES] for k in range(0, WIDE, LANES))
                    if n == 0:
                        square_ref[b, t] = square
                    else:
                        square_ref[b, t] += square
        return carry

    lax.fori_loop(0, groups, embed, 0)

    def place(s, carry):
        base = base_ref[s]
        offset = base % BLOCK
        b = base // BLOCK
        row = lax.broadcasted_iota(jnp.int32, (TILE_ROWS, D), 0)
        for t in range(F_DEV):
            value = jnp.where(row >= offset, h_ref[b, HALO + t], h_ref[b + 1, HALO + t])
            value = pltpu.roll(value, (BLOCK - offset) % BLOCK, 0)
            value = jnp.where(row < rows_ref[s], value, 0.0)
            staged_ref[t, s] = value.astype(jnp.bfloat16)
        pltpu.make_async_copy(staged_ref.at[:, s], out_ref.at[:, s], out_sems.at[s]).start()
        return carry

    for load in loads[4:]:
        load.wait()
    for layer in range(LAYERS):
        gain = gain_row_ref[layer : layer + 1, :]
        for tap in range(3):
            row = conv_row_ref[tap, layer : layer + 1, :] * gain
            coef_ref[layer, tap] = jnp.broadcast_to(row, (BLOCK, D))
        row = conv_bias_row_ref[layer : layer + 1, :]
        coef_ref[layer, 3] = jnp.broadcast_to(row, (BLOCK, D))

    ones = jnp.ones((LANES, LANES), jnp.bfloat16)
    for layer in range(LAYERS):
        start = 2 * layer

        def scales(g, carry, start=start):
            count = FRAMES_IN - start
            these = pl.ds(g * TOGETHER, TOGETHER)
            squares = square_ref[these, start:].reshape(TOGETHER * count * BLOCK, LANES)
            mean = jnp.dot(squares.astype(jnp.bfloat16), ones, preferred_element_type=jnp.float32)
            scale = lax.rsqrt(mean * (1.0 / D) + 1e-06).reshape(TOGETHER, count, BLOCK, LANES)
            for t in range(start, FRAMES_IN):
                scale_ref[these, t] = jnp.where(frame0 + t >= 0, scale[:, t - start], 0.0)
            return carry

        lax.fori_loop(0, (blocks + TOGETHER - 1) // TOGETHER, scales, 0)

        def convolve(b, carry, layer=layer, start=start):
            scale = [scale_ref[b, t] for t in range(start, FRAMES_IN)]

            zeros = jnp.zeros((BLOCK, LANES), jnp.float32)
            squares = [zeros] * (FRAMES_IN - start - 2)
            for n in range(D // LANES):
                cols = slice(n * LANES, (n + 1) * LANES)
                k0, k1, k2, shift = (coef_ref[layer, i, :, cols] for i in range(4))
                two_back = h_ref[b, start, :, cols] * scale[0]
                one_back = h_ref[b, start + 1, :, cols] * scale[1]
                for t in range(start + 2, FRAMES_IN):
                    value = h_ref[b, t, :, cols]
                    normed = value * scale[t - start]
                    mixed = (k0 * normed + k1 * one_back) + (k2 * two_back + shift)
                    value = value + mixed * jax.nn.sigmoid(mixed)
                    h_ref[b, t, :, cols] = value
                    if layer < LAYERS - 1:
                        squares[t - start - 2] = squares[t - start - 2] + value * value
                    two_back, one_back = one_back, normed
            if layer < LAYERS - 1:
                for t in range(start + 2, FRAMES_IN):
                    square_ref[b, t] = squares[t - start - 2]
            return carry

        lax.fori_loop(0, blocks, convolve, 0)

    lax.fori_loop(0, SLOTS_DEV, place, 0)

    def finish(s, carry):
        pltpu.make_async_copy(staged_ref.at[:, s], out_ref.at[:, s], out_sems.at[s]).wait()
        return carry

    lax.fori_loop(0, SLOTS_DEV, finish, 0)


def main_call(sources, chips):
    smem = pl.BlockSpec(memory_space=pltpu.SMEM)
    hbm = pl.BlockSpec(memory_space=pl.ANY)
    vmem = pl.BlockSpec(memory_space=pltpu.VMEM)
    padded = pl.cdiv(MAX_ROWS // BLOCK, TOGETHER) * TOGETHER
    return pl.pallas_call(
        functools.partial(main_kernel, sources),
        out_shape=jax.ShapeDtypeStruct((F_DEV, SLOTS_DEV, TILE_ROWS, D), jnp.bfloat16),
        in_specs=[smem] * 2 + [hbm] * 7,
        out_specs=hbm,
        scratch_shapes=[
            pltpu.SMEM((SLOTS_DEV + 1,), jnp.int32),
            pltpu.SMEM((SLOTS_DEV + 1,), jnp.int32),
            pltpu.VMEM((2, chips, COPIED, TILE_ROWS * PF), jnp.bfloat16),
            pltpu.VMEM((2 * PF, D), jnp.bfloat16),
            pltpu.VMEM((1, D), jnp.float32),
            pltpu.VMEM((LAYERS, D), jnp.float32),
            pltpu.VMEM((3, LAYERS, D), jnp.float32),
            pltpu.VMEM((LAYERS, D), jnp.float32),
            pltpu.VMEM((LAYERS, 4, BLOCK, D), jnp.float32),
            pltpu.VMEM((FRAMES_IN * GROUP, LANES), jnp.bfloat16),
            pltpu.VMEM((MAX_ROWS // BLOCK + 1, FRAMES_IN, BLOCK, D), jnp.float32),
            pltpu.VMEM((padded, FRAMES_IN, BLOCK, LANES), jnp.float32),
            pltpu.VMEM((padded, FRAMES_IN, BLOCK, LANES), jnp.float32),
            pltpu.VMEM((F_DEV, SLOTS_DEV, TILE_ROWS, D), jnp.bfloat16),
            pltpu.SemaphoreType.DMA((7,)),
            pltpu.SemaphoreType.DMA((SLOTS_DEV,)),
        ],
        compiler_params=pltpu.CompilerParams(vmem_limit_bytes=VMEM_LIMIT),
        name="layers",
    )


def per_device(
    patches, owner_list, valid_rows, embed_weight, embed_bias, norm_gain, conv_kernel, conv_bias
):
    sources = lax.axis_size("space")
    chips = lax.axis_size("y")
    smem = pl.BlockSpec(memory_space=pltpu.SMEM)
    vmem = pl.BlockSpec(memory_space=pltpu.VMEM)
    width = TILE_ROWS * PF
    outgoing = pl.pallas_call(
        functools.partial(send_kernel, sources, chips * COPIED),
        out_shape=jax.ShapeDtypeStruct((chips * COPIED, width), jnp.bfloat16),
        in_specs=[smem, vmem],
        out_specs=vmem,
        name="send",
    )(owner_list, patches.reshape(F_DEV * TILES_DEV, width))
    arrived = lax.all_to_all(outgoing, ("y", "space"), split_axis=0, concat_axis=0, tiled=True)
    arrived = arrived.reshape(chips, COPIED, width)
    other = lax.ppermute(arrived, "c", [(0, 1), (1, 0)])
    return main_call(sources, chips)(
        owner_list,
        valid_rows,
        arrived,
        other,
        embed_weight,
        embed_bias.reshape(1, D),
        norm_gain,
        jnp.transpose(conv_kernel, (1, 0, 2)),
        conv_bias,
    )


def solution(mesh):
    frames, space = mesh.shape["tm"], mesh.shape["space"]
    split = Mesh(mesh.devices.reshape(frames // 2, 2, space), ("y", "c", "space"))
    placed = (P(("y", "c"), "space", None), P(), P(), P(), P(), P(), P(), P())
    return jax.shard_map(
        per_device,
        mesh=split,
        in_specs=placed,
        out_specs=P(("y", "c"), "space", None, None),
        check_vma=False,
    )
```
